128 devices in a mesh: dp: 8 (over x, core), feat: 16 (over z, y).
Axes of the slice: x: 4, y: 4, z: 4, core: 2. Of those that a mesh axis runs over, the one named last changes fastest.
Arguments:
- features: bfloat16 [12288, 65536], P('dp', 'feat'), may hold values from -64 to 64
- weight: float32 [16, 65536], P(None, 'feat'), may hold values from -1 to 1
- labels: int32 [12288], P('dp'), may hold values from 0 to 15
- sample_weight: int32 [12288], P('dp'), may hold values from 1 to 4
Outputs:
- logit_step: float32 [12288, 16], P('dp')
- mean_loss: float32 [], replicated
The draws below stay inside these ranges and needn't reach their ends.
All inputs are finite; a program needn't handle non-finite values.
Results may differ from the reference program's by a relative error of at most 0.014.
Values may be sent and summed in bfloat16 or wider, within the bound.
A program may use at most 64 MiB of HBM per device.

```python
import math
import jax
import jax.numpy as jnp

K = 16
CG_ITERS = 4
F = 65536
ROWS = 12288


def draw_weight(key, part):
    normal_part = jax.random.normal(jax.random.fold_in(key, 11), (K, F), dtype=jnp.float32)
    return jnp.clip(normal_part, -4.0, 4.0) * (1.0 / math.sqrt(F))


def draw_features(key, part):
    row_count = ROWS
    row_pos = (jnp.arange(row_count, dtype=jnp.float32) / row_count)[:, None]
    col_pos = (jnp.arange(F, dtype=jnp.float32) / F)[None, :]
    row_scale = jnp.exp(jax.random.uniform(jax.random.fold_in(key, 21), (row_count, 1), jnp.float32, math.log(0.3), math.log(3.0)))
    col_scale = jnp.exp(jax.random.uniform(jax.random.fold_in(key, 22), (1, F), jnp.float32, math.log(0.3), math.log(3.0)))
    ramps = jnp.exp((row_pos - 0.5) * math.log(3.0)) * jnp.exp((col_pos - 0.5) * math.log(3.0))
    normal_part = jnp.clip(jax.random.normal(jax.random.fold_in(key, 29), (row_count, F), dtype=jnp.float32), -4.0, 4.0)
    values = normal_part * row_scale * col_scale * ramps
    return jnp.clip(values, -64.0, 64.0).astype(jnp.bfloat16)


def with_ends(array, stream_key, smallest, high):
    longest = array.shape.index(max(array.shape))
    spots = []
    for shift in (0, 1):
        where = [jax.random.randint(jax.random.fold_in(stream_key, axis), (), 0, length) for axis, length in enumerate(array.shape)]
        where[longest] = (where[longest] + shift) % array.shape[longest]
        spots.append(tuple(where))
    return array.at[spots[0]].set(smallest).at[spots[1]].set(high)


def setup_inputs(seed: int = 0) -> dict:
    splits = jax.random.split(jax.random.key(seed), 5)
    features = draw_features(jax.random.fold_in(splits[4], 71), 0)
    weight = draw_weight(jax.random.fold_in(splits[4], 71), 0)
    labels = with_ends(jax.random.randint(splits[2], (ROWS,), 0, K), jax.random.fold_in(splits[2], 1), 0, K - 1).astype(jnp.int32)
    sample_weight = with_ends(jax.random.randint(splits[3], (ROWS,), 1, 5), jax.random.fold_in(splits[3], 1), 1, 4).astype(jnp.int32)
    return {"features": features, "weight": weight, "labels": labels, "sample_weight": sample_weight}


RIDGE_COEF = 0.1
NORM_GUARD = 1e-6


def reference(features, weight, labels, sample_weight):
    weight_b = weight.astype(jnp.bfloat16)
    logits = jnp.dot(features, weight_b.T, preferred_element_type=jnp.float32)
    row_top = jnp.max(logits, axis=1, keepdims=True)
    shifted = jnp.exp(logits - row_top)
    summed = jnp.sum(shifted, axis=1, keepdims=True)
    class_prob = shifted / summed
    log_total = row_top[:, 0] + jnp.log(summed[:, 0])
    row_weight = sample_weight.astype(jnp.float32)
    weight_total = jnp.sum(row_weight)
    onehot = (labels[:, None] == jnp.arange(K, dtype=jnp.int32)[None, :]).astype(jnp.float32)
    picked = jnp.sum(logits * onehot, axis=1)
    mean_loss = jnp.sum(row_weight * (log_total - picked)) / weight_total
    row_scale = (row_weight / weight_total)[:, None]
    resid_rows = (row_scale * (class_prob - onehot)).astype(jnp.bfloat16)
    gradient = jnp.dot(resid_rows.T, features, preferred_element_type=jnp.float32) + RIDGE_COEF * weight
    newton_step = jnp.zeros_like(gradient)
    residual = -gradient
    direction = residual
    res_norm = jnp.sum(residual * residual)
    for _ in range(CG_ITERS):
        direction_b = direction.astype(jnp.bfloat16)
        dir_scores = jnp.dot(features, direction_b.T, preferred_element_type=jnp.float32)
        mixed_mean = jnp.sum(class_prob * dir_scores, axis=1, keepdims=True)
        curv_rows = (row_scale * class_prob * (dir_scores - mixed_mean)).astype(jnp.bfloat16)
        hess_image = jnp.dot(curv_rows.T, features, preferred_element_type=jnp.float32) + RIDGE_COEF * direction
        step_size = res_norm / jnp.sum(direction * hess_image)
        newton_step = newton_step + step_size * direction
        residual = residual - step_size * hess_image
        new_norm = jnp.sum(residual * residual)
        direction = residual + (new_norm / (res_norm + NORM_GUARD)) * direction
        res_norm = new_norm
    step_b = newton_step.astype(jnp.bfloat16)
    logit_step = jnp.dot(features, step_b.T, preferred_element_type=jnp.float32)
    return logit_step, mean_loss
```

```python
import functools

import jax
import jax.numpy as jnp
from jax import lax
from jax.experimental import pallas as pl
from jax.experimental.pallas import tpu as pltpu
from jax.sharding import PartitionSpec as P

CG_ITERS = 4
RIDGE_COEF = 0.1
NORM_GUARD = 1e-06

RING = 4
CORES = 2
SUBS = 2
LOAD = 6
MESH = pl.DeviceIdType.MESH
F32 = jnp.float32
BF16 = jnp.bfloat16


def dot(a, b, contract_a, contract_b):
    return lax.dot_general(
        a, b, (((contract_a,), (contract_b,)), ((), ())), preferred_element_type=F32
    )


def tile_sum(value):
    total = None
    for i in range(0, value.shape[0], 8):
        for j in range(0, value.shape[1], 128):
            part = value[i : i + 8, j : j + 128]
            total = part if total is None else total + part
    return total


def row_tile_sum(value):
    total = None
    for j in range(0, value.shape[1], 128):
        part = value[:, j : j + 128]
        total = part if total is None else total + part
    first = lax.broadcasted_iota(jnp.int32, (8, 128), 0) == 0
    return jnp.where(first, jnp.broadcast_to(total, (8, 128)), 0.0)


def whole_sum(tile):
    return jnp.sum(jnp.sum(tile, axis=0, keepdims=True), axis=1, keepdims=True)


def ordered_sum(ref, count):
    total = ref[0].astype(F32)
    for i in range(1, count):
        total = total + ref[i].astype(F32)
    return total


def kernel(
    x_hbm,
    w_hbm,
    labels_hbm,
    weights_hbm,
    step_ref,
    loss_ref,
    x_ref,
    xt_ref,
    wb_ref,
    labels_ref,
    weights_ref,
    r_ref,
    d_ref,
    prob_ref,
    rowscale_ref,
    curv_ref,
    sd_ref,
    acc_ref,
    part_ref,
    scal_ref,
    l1_ref,
    l2_ref,
    f1_ref,
    f2_ref,
    g1_ref,
    g2_ref,
    ca_ref,
    cb_ref,
    xs_ref,
    q_ref,
    wt_ref,
    load_sem,
    small_sem,
    l_send,
    l_recv,
    f_send,
    f_recv,
    g_send,
    g_recv,
    ca_send,
    ca_recv,
    cb_send,
    cb_recv,
    xs_send,
    xs_recv,
    q_send,
    q_recv,
    wt_send,
    wt_recv,
):
    dp = lax.axis_index("dp")
    ft = lax.axis_index("feat")
    px, core = dp // CORES, lax.rem(dp, CORES)
    pz, py = ft // RING, lax.rem(ft, RING)
    rows, cols = x_ref.shape
    half = rows // 2
    own_cols = cols // CORES
    sub = own_cols // SUBS
    load_rows = rows // LOAD

    def turn(at, by):
        return lax.rem(at + by, RING)

    def y_peer(k):
        return (dp, pz * RING + turn(py, k))

    def z_peer(k):
        return (dp, turn(pz, k) * RING + py)

    def x_peer(k):
        return (turn(px, k) * CORES + core, ft)

    def dp_peer(k):
        return (lax.rem(dp + k, RING * CORES), ft)

    partner = (px * CORES + (1 - core), ft)

    def load(i):
        start = pl.multiple_of(i * load_rows, load_rows)
        piece = pl.ds(start, load_rows)
        return pltpu.make_async_copy(x_hbm.at[piece], x_ref.at[piece], load_sem.at[i])

    small = [
        pltpu.make_async_copy(w_hbm, d_ref, small_sem.at[0]),
        pltpu.make_async_copy(labels_hbm, labels_ref, small_sem.at[1]),
        pltpu.make_async_copy(weights_hbm, weights_ref, small_sem.at[2]),
    ]
    for copy in small:
        copy.start()
    for i in range(LOAD):
        load(i).start()

    barrier = pltpu.get_barrier_semaphore()
    greeted = [dp_peer(k) for k in range(1, RING * CORES)]
    greeted += [y_peer(k) for k in range(1, RING)] + [z_peer(k) for k in range(1, RING)]
    for peer in greeted:
        pl.semaphore_signal(barrier, inc=1, device_id=peer, device_id_type=MESH)

    for copy in small:
        copy.wait()
    wb_ref[...] = d_ref[...].astype(BF16)
    r_ref[...] = jnp.zeros_like(r_ref)
    sd_ref[...] = jnp.zeros_like(sd_ref)
    step_ref[...] = jnp.zeros_like(step_ref)
    pl.semaphore_wait(barrier, len(greeted))

    def send(src, dst, send_sem, recv_sem, peer):
        copy = pltpu.make_async_remote_copy(
            src_ref=src,
            dst_ref=dst,
            send_sem=send_sem,
            recv_sem=recv_sem,
            device_id=peer,
            device_id_type=MESH,
        )
        copy.start()
        return copy

    def to_dp(ref, send_sem, recv_sem):
        return [
            send(ref.at[dp], ref.at[dp], send_sem.at[k - 1], recv_sem.at[k - 1], dp_peer(k))
            for k in range(1, RING * CORES)
        ]

    def to_ring(ref, at, send_sem, recv_sem, peer):
        return [
            send(ref.at[at], ref.at[at], send_sem.at[k - 1], recv_sem.at[k - 1], peer(k))
            for k in (2, 1, 3)
        ]

    at_1, peer_1 = (py, pz), (y_peer, z_peer)
    at_2, peer_2 = (pz, py), (z_peer, y_peer)

    wt_ref[dp] = row_tile_sum(weights_ref[...].astype(F32))
    wt_copies = to_dp(wt_ref, wt_send, wt_recv)

    def first_scores(i, _):
        load(i).wait()
        start = pl.multiple_of(i * load_rows, load_rows)
        acc_ref[:, pl.ds(start, load_rows)] = dot(
            wb_ref[...], x_ref[pl.ds(start, load_rows), :], 1, 1
        )
        return 0

    lax.fori_loop(0, LOAD, first_scores, 0)

    def turn_over(first, last):
        block = 512
        per_row = cols // block

        def one(i, _):
            row = pl.multiple_of((i // per_row) * block, block)
            col = pl.multiple_of(lax.rem(i, per_row) * block, block)
            xt_ref[pl.ds(col, block), pl.ds(row, block)] = x_ref[
                pl.ds(row, block), pl.ds(col, block)
            ].T
            return 0

        lax.fori_loop(first, last, one, 0)

    blocks = (rows // 512) * (cols // 512)

    copies_1 = []
    for h in range(2):
        l1_ref[h, at_1[h]] = acc_ref[:, h * half : (h + 1) * half]
        copies_1 += to_ring(l1_ref.at[h], at_1[h], l_send.at[0, h], l_recv.at[0, h], peer_1[h])
    turn_over(0, blocks // 2)
    copies_2 = []
    for h in range(2):
        for copy in copies_1[3 * h : 3 * h + 3]:
            copy.wait_recv()
        l2_ref[h, at_2[h]] = ordered_sum(l1_ref.at[h], RING)
        copies_2 += to_ring(l2_ref.at[h], at_2[h], l_send.at[1, h], l_recv.at[1, h], peer_2[h])
    turn_over(blocks // 2, blocks)
    for copy in wt_copies:
        copy.wait()
    weight_total = whole_sum(ordered_sum(wt_ref, RING * CORES))

    loss_tile = None
    classes = lax.broadcasted_iota(jnp.int32, (w_hbm.shape[0], half), 0)
    for h in range(2):
        for copy in copies_2[3 * h : 3 * h + 3]:
            copy.wait_recv()
        at = slice(h * half, (h + 1) * half)
        logits = ordered_sum(l2_ref.at[h], RING)
        row_top = jnp.max(logits, axis=0, keepdims=True)
        shifted = jnp.exp(logits - row_top)
        summed = jnp.sum(shifted, axis=0, keepdims=True)
        class_prob = shifted / summed
        log_total = row_top + jnp.log(summed)
        row_weight = weights_ref[:, at].astype(F32)
        onehot = (labels_ref[:, at] == classes).astype(F32)
        picked = jnp.sum(logits * onehot, axis=0, keepdims=True)
        part = row_tile_sum(row_weight * (log_total - picked))
        loss_tile = part if loss_tile is None else loss_tile + part
        row_scale = row_weight / weight_total
        prob_ref[:, at] = class_prob
        rowscale_ref[:, at] = row_scale
        curv_ref[:, at] = (row_scale * (class_prob - onehot)).astype(BF16)
    for copy in copies_1 + copies_2:
        copy.wait_send()

    q_ref[0, dp] = loss_tile
    to_dp(q_ref.at[0], q_send.at[0], q_recv.at[0])

    def wait_dp(slot):
        for k in range(1, RING * CORES):
            pltpu.make_async_remote_copy(
                src_ref=q_ref.at[slot, dp],
                dst_ref=q_ref.at[slot, dp],
                send_sem=q_send.at[slot, k - 1],
                recv_sem=q_recv.at[slot, k - 1],
                device_id=dp_peer(k),
                device_id_type=MESH,
            ).wait()
        return whole_sum(ordered_sum(q_ref.at[slot], RING * CORES))

    one = jnp.ones((8, 128), F32)
    scal_ref[0] = one
    scal_ref[1] = one
    scal_ref[2] = one
    mine = core * own_cols
    theirs = (1 - core) * own_cols

    def iteration(it, _):
        slot = lax.rem(it, 2)

        ca_copies = []
        for s in range(SUBS):
            start = pl.multiple_of(theirs + s * sub, sub)
            ca_ref[slot, 0, s] = dot(curv_ref[...], x_ref[:, pl.ds(start, sub)], 1, 0).astype(BF16)
            ca_copies.append(
                send(
                    ca_ref.at[slot, 0, s],
                    ca_ref.at[slot, 1, s],
                    ca_send.at[slot, s],
                    ca_recv.at[slot, s],
                    partner,
                )
            )
        xs_copies = []
        for s in range(SUBS):
            start = pl.multiple_of(mine + s * sub, sub)
            part = dot(curv_ref[...], x_ref[:, pl.ds(start, sub)], 1, 0)
            ca_copies[s].wait_recv()
            xs_ref[slot, s, px] = (part + ca_ref[slot, 1, s].astype(F32)).astype(BF16)
            xs_copies.append(
                to_ring(
                    xs_ref.at[slot, s], px, xs_send.at[slot, s], xs_recv.at[slot, s], x_peer
                )
            )

        reduced = wait_dp(slot)
        beta = scal_ref[0, 0:1, 0:1]
        res_norm = scal_ref[1, 0:1, 0:1]
        dir_norm = scal_ref[2, 0:1, 0:1]
        first = it == 0

        @pl.when(first)
        def _():
            loss_ref[...] = reduced / weight_total

        step_size = jnp.where(first, 1.0, res_norm / (reduced + RIDGE_COEF * dir_norm))
        step_ref[...] = step_ref[...] + step_size * sd_ref[...]

        def advance(start, image, tiles):
            at = pl.ds(pl.multiple_of(start, sub), sub)
            residual = r_ref[:, at]
            direction = residual + beta * d_ref[:, at]
            residual = residual - step_size * (image.astype(F32) + RIDGE_COEF * direction)
            r_ref[:, at] = residual
            d_ref[:, at] = direction
            scores = dot(residual.astype(BF16), xt_ref[at, :], 1, 0)
            both = (tile_sum(residual * residual), tile_sum(residual * direction))
            return scores, both if tiles is None else tuple(a + b for a, b in zip(tiles, both))

        cb_copies = []
        tiles = None
        for s in range(SUBS):
            for copy in xs_copies[s]:
                copy.wait_recv()
            cb_ref[slot, 0, s] = ordered_sum(xs_ref.at[slot, s], RING).astype(BF16)
            cb_copies.append(
                send(
                    cb_ref.at[slot, 0, s],
                    cb_ref.at[slot, 1, s],
                    cb_send.at[slot, s],
                    cb_recv.at[slot, s],
                    partner,
                )
            )
            scores, tiles = advance(mine + s * sub, cb_ref[slot, 0, s], tiles)
            acc_ref[...] = scores if s == 0 else acc_ref[...] + scores
        for s in range(SUBS):
            cb_copies[s].wait_recv()
            scores, tiles = advance(theirs + s * sub, cb_ref[slot, 1, s], tiles)
            acc_ref[...] = acc_ref[...] + scores

        copies_1, copies_2 = [], []
        g1_ref[slot, py, 0] = tiles[0]
        g1_ref[slot, py, 1] = tiles[1]
        for h in range(2):
            f1_ref[slot, h, at_1[h]] = acc_ref[:, h * half : (h + 1) * half].astype(BF16)
            copies_1 += to_ring(
                f1_ref.at[slot, h], at_1[h], f_send.at[slot, 0, h], f_recv.at[slot, 0, h], peer_1[h]
            )
        small_1 = to_ring(g1_ref.at[slot], py, g_send.at[slot, 0], g_recv.at[slot, 0], y_peer)
        for h in range(2):
            for copy in copies_1[3 * h : 3 * h + 3]:
                copy.wait_recv()
            f2_ref[slot, h, at_2[h]] = ordered_sum(f1_ref.at[slot, h], RING).astype(BF16)
            copies_2 += to_ring(
                f2_ref.at[slot, h], at_2[h], f_send.at[slot, 1, h], f_recv.at[slot, 1, h], peer_2[h]
            )
        for copy in small_1:
            copy.wait_recv()
        g2_ref[slot, pz] = ordered_sum(g1_ref.at[slot], RING)
        small_2 = to_ring(g2_ref.at[slot], pz, g_send.at[slot, 1], g_recv.at[slot, 1], z_peer)
        for copies in xs_copies:
            for copy in copies:
                copy.wait_send()
        for copy in ca_copies + cb_copies + copies_1 + small_1:
            copy.wait_send()

        for copy in small_2:
            copy.wait()
        sums = ordered_sum(g2_ref.at[slot], RING)
        new_norm = whole_sum(sums[0])
        cross = whole_sum(sums[1])
        new_beta = jnp.where(first, 0.0, new_norm / (res_norm + NORM_GUARD))
        new_dir_norm = new_norm + new_beta * (2.0 * cross + new_beta * dir_norm)
        scal_ref[0] = jnp.broadcast_to(new_beta, (8, 128))
        scal_ref[1] = jnp.broadcast_to(new_norm, (8, 128))
        scal_ref[2] = jnp.broadcast_to(new_dir_norm, (8, 128))
        curvature = None
        for h in range(2):
            for copy in copies_2[3 * h : 3 * h + 3]:
                copy.wait()
            at = slice(h * half, (h + 1) * half)
            scores = ordered_sum(f2_ref.at[slot, h], RING) + new_beta * sd_ref[:, at]
            sd_ref[:, at] = scores
            class_prob = prob_ref[:, at]
            mixed = jnp.sum(class_prob * scores, axis=0, keepdims=True)
            curv = (rowscale_ref[:, at] * class_prob * (scores - mixed)).astype(BF16)
            curv_ref[:, at] = curv
            part = tile_sum(scores * curv.astype(F32))
            curvature = part if curvature is None else curvature + part
        q_ref[1 - slot, dp] = curvature
        to_dp(q_ref.at[1 - slot], q_send.at[1 - slot], q_recv.at[1 - slot])
        return 0

    lax.fori_loop(0, CG_ITERS, iteration, 0)

    last = CG_ITERS % 2
    reduced = wait_dp(last)
    step_size = scal_ref[1, 0:1, 0:1] / (reduced + RIDGE_COEF * scal_ref[2, 0:1, 0:1])
    step_ref[...] = step_ref[...] + step_size * sd_ref[...]


def on_device(features, weight, labels, sample_weight):
    rows, cols = features.shape
    classes = weight.shape[0]
    half, sub = rows // 2, cols // CORES // SUBS
    any_space = pl.BlockSpec(memory_space=pl.ANY)
    vmem = pl.BlockSpec(memory_space=pltpu.VMEM)
    dma = pltpu.SemaphoreType.DMA
    peers = RING * CORES - 1
    step, loss = pl.pallas_call(
        kernel,
        out_shape=(
            jax.ShapeDtypeStruct((classes, rows), F32),
            jax.ShapeDtypeStruct((1, 1), F32),
        ),
        in_specs=[any_space] * 4,
        out_specs=(vmem, vmem),
        scratch_shapes=[
            pltpu.VMEM((rows, cols), BF16),
            pltpu.VMEM((cols, rows), BF16),
            pltpu.VMEM((classes, cols), BF16),
            pltpu.VMEM((1, rows), jnp.int32),
            pltpu.VMEM((1, rows), jnp.int32),
            pltpu.VMEM((classes, cols), F32),
            pltpu.VMEM((classes, cols), F32),
            pltpu.VMEM((classes, rows), F32),
            pltpu.VMEM((1, rows), F32),
            pltpu.VMEM((classes, rows), BF16),
            pltpu.VMEM((classes, rows), F32),
            pltpu.VMEM((classes, rows), F32),
            pltpu.VMEM((classes, sub), F32),
            pltpu.VMEM((3, 8, 128), F32),
            pltpu.VMEM((2, RING, classes, half), F32),
            pltpu.VMEM((2, RING, classes, half), F32),
            pltpu.VMEM((2, 2, RING, classes, half), BF16),
            pltpu.VMEM((2, 2, RING, classes, half), BF16),
            pltpu.VMEM((2, RING, 2, 8, 128), F32),
            pltpu.VMEM((2, RING, 2, 8, 128), F32),
            pltpu.VMEM((2, 2, SUBS, classes, sub), BF16),
            pltpu.VMEM((2, 2, SUBS, classes, sub), BF16),
            pltpu.VMEM((2, SUBS, RING, classes, sub), BF16),
            pltpu.VMEM((2, RING * CORES, 8, 128), F32),
            pltpu.VMEM((RING * CORES, 8, 128), F32),
            dma((LOAD,)),
            dma((3,)),
            dma((2, 2, 3)),
            dma((2, 2, 3)),
            dma((2, 2, 2, 3)),
            dma((2, 2, 2, 3)),
            dma((2, 2, 3)),
            dma((2, 2, 3)),
            dma((2, SUBS)),
            dma((2, SUBS)),
            dma((2, SUBS)),
            dma((2, SUBS)),
            dma((2, SUBS, 3)),
            dma((2, SUBS, 3)),
            dma((2, peers)),
            dma((2, peers)),
            dma((peers,)),
            dma((peers,)),
        ],
        compiler_params=pltpu.CompilerParams(
            collective_id=0, has_side_effects=True, vmem_limit_bytes=56 * 1024 * 1024
        ),
        name="newton_cg",
    )(features, weight, labels.reshape(1, rows), sample_weight.reshape(1, rows))
    return step.T, loss.reshape(())


def solution(mesh):
    in_specs = (P("dp", "feat"), P(None, "feat"), P("dp"), P("dp"))
    out_specs = (P("dp", None), P())
    return jax.shard_map(
        on_device, mesh=mesh, in_specs=in_specs, out_specs=out_specs, check_vma=False
    )
```

```python
import functools

import jax
import jax.numpy as jnp
from jax import lax
from jax.experimental import pallas as pl
from jax.experimental.pallas import tpu as pltpu
from jax.sharding import PartitionSpec as P

CG_ITERS = 4
RIDGE_COEF = 0.1
NORM_GUARD = 1e-06

RING = 4
CORES = 2
SUBS = (512, 1024, 512)
LOAD = (256, 512, 256, 512)
EARLY = 2
MESH = pl.DeviceIdType.MESH
F32 = jnp.float32
BF16 = jnp.bfloat16


def dot(a, b, contract_a, contract_b):
    return lax.dot_general(
        a, b, (((contract_a,), (contract_b,)), ((), ())), preferred_element_type=F32
    )


def tile_sum(value):
    total = None
    for i in range(0, value.shape[0], 8):
        for j in range(0, value.shape[1], 128):
            part = value[i : i + 8, j : j + 128]
            total = part if total is None else total + part
    return total


def row_tile_sum(value):
    total = None
    for j in range(0, value.shape[1], 128):
        part = value[:, j : j + 128]
        total = part if total is None else total + part
    first = lax.broadcasted_iota(jnp.int32, (8, 128), 0) == 0
    return jnp.where(first, jnp.broadcast_to(total, (8, 128)), 0.0)


def whole_sum(tile):
    return jnp.sum(jnp.sum(tile, axis=0, keepdims=True), axis=1, keepdims=True)


def row_of(ref, start, size):
    return ref[start : start + size].reshape(1, size)


def ordered_sum(ref, count):
    total = ref[0].astype(F32)
    for i in range(1, count):
        total = total + ref[i].astype(F32)
    return total


def kernel(
    x_hbm,
    w_hbm,
    labels_hbm,
    weights_hbm,
    step_ref,
    loss_hbm,
    x_ref,
    xt_ref,
    wb_ref,
    labels_ref,
    weights_ref,
    loss_ref,
    r_ref,
    d_ref,
    prob_ref,
    rowscale_ref,
    curv_ref,
    sd_ref,
    acc_ref,
    scal_ref,
    l1_ref,
    l2_ref,
    f1_ref,
    f2_ref,
    g1_ref,
    g2_ref,
    ca_ref,
    cb_ref,
    xs_ref,
    q_ref,
    wt_ref,
    load_sem,
    small_sem,
    l_send,
    l_recv,
    f_send,
    f_recv,
    g_send,
    g_recv,
    ca_send,
    ca_recv,
    cb_send,
    cb_recv,
    xs_send,
    xs_recv,
    q_send,
    q_recv,
    wt_send,
    wt_recv,
):
    dp = lax.axis_index("dp")
    ft = lax.axis_index("feat")
    px, core = dp // CORES, lax.rem(dp, CORES)
    pz, py = ft // RING, lax.rem(ft, RING)
    rows, cols = x_ref.shape
    half = rows // 2
    own_cols = cols // CORES
    pieces = [(sum(SUBS[:s]), SUBS[s]) for s in range(len(SUBS))]

    def turn(at, by):
        return lax.rem(at + by, RING)

    def y_peer(k):
        return (dp, pz * RING + turn(py, k))

    def z_peer(k):
        return (dp, turn(pz, k) * RING + py)

    def x_peer(k):
        return (turn(px, k) * CORES + core, ft)

    def dp_peer(k):
        return (lax.rem(dp + k, RING * CORES), ft)

    partner = (px * CORES + (1 - core), ft)

    def load(i):
        piece = pl.ds(sum(LOAD[:i]), LOAD[i])
        return pltpu.make_async_copy(x_hbm.at[piece], x_ref.at[piece], load_sem.at[i])

    small = [
        pltpu.make_async_copy(w_hbm, d_ref, small_sem.at[0]),
        pltpu.make_async_copy(labels_hbm, labels_ref, small_sem.at[1]),
        pltpu.make_async_copy(weights_hbm, weights_ref, small_sem.at[2]),
    ]
    store_loss = pltpu.make_async_copy(loss_ref, loss_hbm, small_sem.at[3])
    small[0].start()
    for i in range(EARLY):
        load(i).start()
    small[1].start()
    small[2].start()

    barrier = pltpu.get_barrier_semaphore()
    greeted = [dp_peer(k) for k in range(1, RING * CORES)]
    greeted += [y_peer(k) for k in range(1, RING)] + [z_peer(k) for k in range(1, RING)]
    for peer in greeted:
        pl.semaphore_signal(barrier, inc=1, device_id=peer, device_id_type=MESH)

    small[0].wait()
    for i in range(EARLY, len(LOAD)):
        load(i).start()
    wb_ref[...] = d_ref[...].astype(BF16)
    r_ref[...] = jnp.zeros_like(r_ref)
    sd_ref[...] = jnp.zeros_like(sd_ref)
    step_ref[...] = jnp.zeros_like(step_ref)
    def send(src, dst, send_sem, recv_sem, peer):
        copy = pltpu.make_async_remote_copy(
            src_ref=src,
            dst_ref=dst,
            send_sem=send_sem,
            recv_sem=recv_sem,
            device_id=peer,
            device_id_type=MESH,
        )
        copy.start()
        return copy

    def to_dp(ref, send_sem, recv_sem):
        for k in range(1, RING * CORES):
            send(ref.at[dp], ref.at[dp], send_sem, recv_sem, dp_peer(k))

    def to_ring(ref, at, send_sem, recv_sem, peer):
        for k in (2, 1, 3):
            send(ref.at[at], ref.at[at], send_sem, recv_sem, peer(k))

    def wait_group(ref, sem):
        others = ref.at[pl.ds(0, ref.shape[0] - 1)]
        pltpu.make_async_copy(others, others, sem).wait()

    at_1, peer_1 = (py, pz), (y_peer, z_peer)
    at_2, peer_2 = (pz, py), (z_peer, y_peer)

    for i in range(len(LOAD)):
        start = sum(LOAD[:i])
        load(i).wait()
        h, into = divmod(start, half)
        l1_ref[h, at_1[h], :, into : into + LOAD[i]] = dot(
            wb_ref[...], x_ref[start : start + LOAD[i], :], 1, 1
        )
        if into + LOAD[i] == half:
            if h == 0:
                pl.semaphore_wait(barrier, len(greeted))
            to_ring(l1_ref.at[h], at_1[h], l_send.at[0, h], l_recv.at[0, h], peer_1[h])
    small[1].wait()
    small[2].wait()
    wt_ref[dp] = row_tile_sum(row_of(weights_ref, 0, rows).astype(F32))
    to_dp(wt_ref, wt_send.at[0], wt_recv.at[0])

    def turn_over(first, last):
        block = 512
        per_row = cols // block

        def one(i, _):
            row = pl.multiple_of((i // per_row) * block, block)
            col = pl.multiple_of(lax.rem(i, per_row) * block, block)
            xt_ref[pl.ds(col, block), pl.ds(row, block)] = x_ref[
                pl.ds(row, block), pl.ds(col, block)
            ].T
            return 0

        lax.fori_loop(first, last, one, 0)

    blocks = (rows // 512) * (cols // 512)

    turn_over(0, blocks // 2)
    for h in range(2):
        wait_group(l1_ref.at[h], l_recv.at[0, h])
        l2_ref[h, at_2[h]] = ordered_sum(l1_ref.at[h], RING)
        to_ring(l2_ref.at[h], at_2[h], l_send.at[1, h], l_recv.at[1, h], peer_2[h])
    turn_over(blocks // 2, blocks)
    wait_group(wt_ref, wt_recv.at[0])
    weight_total = whole_sum(ordered_sum(wt_ref, RING * CORES))

    loss_tile = None
    classes = lax.broadcasted_iota(jnp.int32, (w_hbm.shape[0], half), 0)
    for h in range(2):
        wait_group(l2_ref.at[h], l_recv.at[1, h])
        at = slice(h * half, (h + 1) * half)
        logits = ordered_sum(l2_ref.at[h], RING)
        row_top = jnp.max(logits, axis=0, keepdims=True)
        shifted = jnp.exp(logits - row_top)
        summed = jnp.sum(shifted, axis=0, keepdims=True)
        class_prob = shifted / summed
        log_total = row_top + jnp.log(summed)
        row_weight = row_of(weights_ref, h * half, half).astype(F32)
        onehot = (row_of(labels_ref, h * half, half) == classes).astype(F32)
        picked = jnp.sum(logits * onehot, axis=0, keepdims=True)
        part = row_tile_sum(row_weight * (log_total - picked))
        loss_tile = part if loss_tile is None else loss_tile + part
        row_scale = row_weight / weight_total
        prob_ref[:, at] = class_prob
        rowscale_ref[:, at] = row_scale
        curv_ref[:, at] = (row_scale * (class_prob - onehot)).astype(BF16)
    q_ref[0, dp] = loss_tile
    to_dp(q_ref.at[0], q_send.at[0], q_recv.at[0])
    for h in range(2):
        wait_group(l1_ref.at[h], l_send.at[0, h])
        wait_group(l2_ref.at[h], l_send.at[1, h])
    wait_group(wt_ref, wt_send.at[0])

    def wait_dp(slot):
        wait_group(q_ref.at[slot], q_recv.at[slot])
        wait_group(q_ref.at[slot], q_send.at[slot])
        return whole_sum(ordered_sum(q_ref.at[slot], RING * CORES))

    one = jnp.ones((8, 128), F32)
    scal_ref[0] = one
    scal_ref[1] = one
    scal_ref[2] = one
    mine = core * own_cols
    theirs = (1 - core) * own_cols

    def iteration(it, _):
        slot = lax.rem(it, 2)

        ca_copies = []
        for s, (at, size) in enumerate(pieces):
            start = pl.multiple_of(theirs + at, 128)
            piece = pl.ds(at, size)
            ca_ref[slot, 0, :, piece] = dot(curv_ref[...], x_ref[:, pl.ds(start, size)], 1, 0).astype(
                BF16
            )
            ca_copies.append(
                send(
                    ca_ref.at[slot, 0, :, piece],
                    ca_ref.at[slot, 1, :, piece],
                    ca_send.at[slot, s],
                    ca_recv.at[slot, s],
                    partner,
                )
            )
        for s, (at, size) in enumerate(pieces):
            start = pl.multiple_of(mine + at, 128)
            piece = pl.ds(at, size)
            part = dot(curv_ref[...], x_ref[:, pl.ds(start, size)], 1, 0)
            ca_copies[s].wait_recv()
            xs_ref[slot, px, :, piece] = (part + ca_ref[slot, 1, :, piece].astype(F32)).astype(BF16)
            to_ring(
                xs_ref.at[slot, :, :, piece], px, xs_send.at[slot, s], xs_recv.at[slot, s], x_peer
            )

        reduced = wait_dp(slot)
        beta = scal_ref[0, 0:1, 0:1]
        res_norm = scal_ref[1, 0:1, 0:1]
        dir_norm = scal_ref[2, 0:1, 0:1]
        first = it == 0

        @pl.when(first)
        def _():
            loss_ref[...] = reduced / weight_total
            store_loss.start()

        step_size = jnp.where(first, 1.0, res_norm / (reduced + RIDGE_COEF * dir_norm))
        step_ref[...] = step_ref[...] + step_size * sd_ref[...]

        def advance(start, size, image):
            at = pl.ds(pl.multiple_of(start, 128), size)
            residual = r_ref[:, at]
            direction = residual + beta * d_ref[:, at]
            residual = residual - step_size * (image.astype(F32) + RIDGE_COEF * direction)
            r_ref[:, at] = residual
            d_ref[:, at] = direction
            tiles.append((tile_sum(residual * residual), tile_sum(residual * direction)))
            return residual.astype(BF16), xt_ref.at[at]

        tiles = []
        cb_copies = []
        for s, (at, size) in enumerate(pieces):
            piece = pl.ds(at, size)
            wait_group(xs_ref.at[slot, :, :, piece], xs_recv.at[slot, s])
            image = ordered_sum(xs_ref.at[slot, :, :, piece], RING).astype(BF16)
            cb_ref[slot, 0, :, piece] = image
            cb_copies.append(
                send(
                    cb_ref.at[slot, 0, :, piece],
                    cb_ref.at[slot, 1, :, piece],
                    cb_send.at[slot, s],
                    cb_recv.at[slot, s],
                    partner,
                )
            )
            residual, turned = advance(mine + at, size, image)
            scores = dot(residual, turned[...], 1, 0)
            acc_ref[...] = scores if s == 0 else acc_ref[...] + scores
        for s, (at, size) in enumerate(pieces):
            cb_copies[s].wait_recv()
            residual, turned = advance(theirs + at, size, cb_ref[slot, 1, :, pl.ds(at, size)])
            if s < len(pieces) - 1:
                acc_ref[...] = acc_ref[...] + dot(residual, turned[...], 1, 0)

        for i in range(2):
            total = tiles[0][i]
            for both in tiles[1:]:
                total = total + both[i]
            g1_ref[slot, py, i] = total
        to_ring(g1_ref.at[slot], py, g_send.at[slot, 0], g_recv.at[slot, 0], y_peer)
        for h in range(2):
            at = slice(h * half, (h + 1) * half)
            f1_ref[slot, h, at_1[h]] = (acc_ref[:, at] + dot(residual, turned[:, at], 1, 0)).astype(
                BF16
            )
            to_ring(
                f1_ref.at[slot, h], at_1[h], f_send.at[slot, 0, h], f_recv.at[slot, 0, h], peer_1[h]
            )
        wait_group(g1_ref.at[slot], g_recv.at[slot, 0])
        g2_ref[slot, pz] = ordered_sum(g1_ref.at[slot], RING)
        to_ring(g2_ref.at[slot], pz, g_send.at[slot, 1], g_recv.at[slot, 1], z_peer)
        for h in range(2):
            wait_group(f1_ref.at[slot, h], f_recv.at[slot, 0, h])
            f2_ref[slot, h, at_2[h]] = ordered_sum(f1_ref.at[slot, h], RING).astype(BF16)
            to_ring(
                f2_ref.at[slot, h], at_2[h], f_send.at[slot, 1, h], f_recv.at[slot, 1, h], peer_2[h]
            )
        for s, (at, size) in enumerate(pieces):
            wait_group(xs_ref.at[slot, :, :, pl.ds(at, size)], xs_send.at[slot, s])
        for copy in ca_copies + cb_copies:
            copy.wait_send()
        for h in range(2):
            wait_group(f1_ref.at[slot, h], f_send.at[slot, 0, h])
        wait_group(g1_ref.at[slot], g_send.at[slot, 0])

        wait_group(g2_ref.at[slot], g_recv.at[slot, 1])
        wait_group(g2_ref.at[slot], g_send.at[slot, 1])
        sums = ordered_sum(g2_ref.at[slot], RING)
        new_norm = whole_sum(sums[0])
        cross = whole_sum(sums[1])
        new_beta = jnp.where(first, 0.0, new_norm / (res_norm + NORM_GUARD))
        new_dir_norm = new_norm + new_beta * (2.0 * cross + new_beta * dir_norm)
        scal_ref[0] = jnp.broadcast_to(new_beta, (8, 128))
        scal_ref[1] = jnp.broadcast_to(new_norm, (8, 128))
        scal_ref[2] = jnp.broadcast_to(new_dir_norm, (8, 128))
        curvature = None
        for h in range(2):
            wait_group(f2_ref.at[slot, h], f_recv.at[slot, 1, h])
            at = slice(h * half, (h + 1) * half)
            scores = ordered_sum(f2_ref.at[slot, h], RING) + new_beta * sd_ref[:, at]
            sd_ref[:, at] = scores
            class_prob = prob_ref[:, at]
            mixed = jnp.sum(class_prob * scores, axis=0, keepdims=True)
            curv = (rowscale_ref[:, at] * class_prob * (scores - mixed)).astype(BF16)
            curv_ref[:, at] = curv
            part = tile_sum(scores * curv.astype(F32))
            curvature = part if curvature is None else curvature + part
        q_ref[1 - slot, dp] = curvature
        to_dp(q_ref.at[1 - slot], q_send.at[1 - slot], q_recv.at[1 - slot])
        for h in range(2):
            wait_group(f2_ref.at[slot, h], f_send.at[slot, 1, h])
        return 0

    lax.fori_loop(0, CG_ITERS, iteration, 0)

    store_loss.wait()
    last = CG_ITERS % 2
    reduced = wait_dp(last)
    step_size = scal_ref[1, 0:1, 0:1] / (reduced + RIDGE_COEF * scal_ref[2, 0:1, 0:1])
    step_ref[...] = step_ref[...] + step_size * sd_ref[...]


def on_device(features, weight, labels, sample_weight):
    arrays = (features, weight, labels, sample_weight)
    rows, cols = features.shape
    classes = weight.shape[0]
    half, own_cols = rows // 2, cols // CORES
    hbm = pl.BlockSpec(memory_space=pltpu.HBM)
    vmem = pl.BlockSpec(memory_space=pltpu.VMEM)
    dma = pltpu.SemaphoreType.DMA
    subs = len(SUBS)
    step, loss = pl.pallas_call(
        kernel,
        out_shape=(
            jax.ShapeDtypeStruct((classes, rows), F32),
            jax.ShapeDtypeStruct((1, 1), F32),
        ),
        in_specs=[hbm] * 4,
        out_specs=(vmem, hbm),
        scratch_shapes=[
            pltpu.VMEM((rows, cols), BF16),
            pltpu.VMEM((cols, rows), BF16),
            pltpu.VMEM((classes, cols), BF16),
            pltpu.VMEM((rows,), jnp.int32),
            pltpu.VMEM((rows,), jnp.int32),
            pltpu.VMEM((1, 1), F32),
            pltpu.VMEM((classes, cols), F32),
            pltpu.VMEM((classes, cols), F32),
            pltpu.VMEM((classes, rows), F32),
            pltpu.VMEM((1, rows), F32),
            pltpu.VMEM((classes, rows), BF16),
            pltpu.VMEM((classes, rows), F32),
            pltpu.VMEM((classes, rows), F32),
            pltpu.VMEM((3, 8, 128), F32),
            pltpu.VMEM((2, RING, classes, half), F32),
            pltpu.VMEM((2, RING, classes, half), F32),
            pltpu.VMEM((2, 2, RING, classes, half), BF16),
            pltpu.VMEM((2, 2, RING, classes, half), BF16),
            pltpu.VMEM((2, RING, 2, 8, 128), F32),
            pltpu.VMEM((2, RING, 2, 8, 128), F32),
            pltpu.VMEM((2, 2, classes, own_cols), BF16),
            pltpu.VMEM((2, 2, classes, own_cols), BF16),
            pltpu.VMEM((2, RING, classes, own_cols), BF16),
            pltpu.VMEM((2, RING * CORES, 8, 128), F32),
            pltpu.VMEM((RING * CORES, 8, 128), F32),
            dma((len(LOAD),)),
            dma((4,)),
            dma((2, 2)),
            dma((2, 2)),
            dma((2, 2, 2)),
            dma((2, 2, 2)),
            dma((2, 2)),
            dma((2, 2)),
            dma((2, subs)),
            dma((2, subs)),
            dma((2, subs)),
            dma((2, subs)),
            dma((2, subs)),
            dma((2, subs)),
            dma((2,)),
            dma((2,)),
            dma((1,)),
            dma((1,)),
        ],
        compiler_params=pltpu.CompilerParams(
            collective_id=0, has_side_effects=True, vmem_limit_bytes=44 * 1024 * 1024
        ),
        name="newton_cg",
    )(*(pltpu.with_memory_space_constraint(a, pltpu.HBM) for a in arrays))
    return step.T, loss.reshape(())


def solution(mesh):
    in_specs = (P("dp", "feat"), P(None, "feat"), P("dp"), P("dp"))
    out_specs = (P("dp", None), P())
    return jax.shard_map(
        on_device, mesh=mesh, in_specs=in_specs, out_specs=out_specs, check_vma=False
    )
```

```python
import functools

import jax
import jax.numpy as jnp
from jax import lax
from jax.experimental import pallas as pl
from jax.experimental.pallas import tpu as pltpu
from jax.sharding import PartitionSpec as P

CG_ITERS = 4
RIDGE_COEF = 0.1
NORM_GUARD = 1e-06

RING = 4
CORES = 2
SUBS = (512, 1024, 512)
BLOCK = 512
WIDE = 2
EARLY = 2
MESH = pl.DeviceIdType.MESH
F32 = jnp.float32
BF16 = jnp.bfloat16


def dot(a, b, contract_a, contract_b):
    return lax.dot_general(
        a, b, (((contract_a,), (contract_b,)), ((), ())), preferred_element_type=F32
    )


def tile_sum(value):
    total = None
    for i in range(0, value.shape[0], 8):
        for j in range(0, value.shape[1], 128):
            part = value[i : i + 8, j : j + 128]
            total = part if total is None else total + part
    return total


def row_tile_sum(value):
    total = None
    for j in range(0, value.shape[1], 128):
        part = value[:, j : j + 128]
        total = part if total is None else total + part
    first = lax.broadcasted_iota(jnp.int32, (8, 128), 0) == 0
    return jnp.where(first, jnp.broadcast_to(total, (8, 128)), 0.0)


def whole_sum(tile):
    return jnp.sum(jnp.sum(tile, axis=0, keepdims=True), axis=1, keepdims=True)


def row_of(ref, start, size):
    return ref[start : start + size].reshape(1, size)


def ordered_sum(ref, count):
    total = ref[0].astype(F32)
    for i in range(1, count):
        total = total + ref[i].astype(F32)
    return total


def kernel(
    x_hbm,
    w_hbm,
    labels_hbm,
    weights_hbm,
    step_ref,
    loss_hbm,
    x_ref,
    xt_ref,
    wb_ref,
    labels_ref,
    weights_ref,
    loss_ref,
    r_ref,
    d_ref,
    prob_ref,
    rowscale_ref,
    curv_ref,
    sd_ref,
    acc_ref,
    part_ref,
    scal_ref,
    l1_ref,
    l2_ref,
    f1_ref,
    f2_ref,
    g1_ref,
    g2_ref,
    ca_ref,
    cb_ref,
    xs_ref,
    q_ref,
    wt_ref,
    load_sem,
    small_sem,
    f_send,
    f_recv,
    g_send,
    g_recv,
    ca_send,
    ca_recv,
    cb_send,
    cb_recv,
    xs_send,
    xs_recv,
    q_send,
    q_recv,
    wt_send,
    wt_recv,
):
    dp = lax.axis_index("dp")
    ft = lax.axis_index("feat")
    px, core = dp // CORES, lax.rem(dp, CORES)
    pz, py = ft // RING, lax.rem(ft, RING)
    rows, cols = x_ref.shape
    half = rows // 2
    own_cols = cols // CORES
    wide = cols // WIDE
    loads = rows // BLOCK * WIDE
    pieces = [(sum(SUBS[:s]), SUBS[s]) for s in range(len(SUBS))]

    def turn(at, by):
        return lax.rem(at + by, RING)

    def y_peer(k):
        return (dp, pz * RING + turn(py, k))

    def z_peer(k):
        return (dp, turn(pz, k) * RING + py)

    def x_peer(k):
        return (turn(px, k) * CORES + core, ft)

    def dp_peer(k):
        return (lax.rem(dp + k, RING * CORES), ft)

    partner = (px * CORES + (1 - core), ft)

    def load(i):
        at = pl.ds(i // WIDE * BLOCK, BLOCK), pl.ds(i % WIDE * wide, wide)
        return pltpu.make_async_copy(x_hbm.at[at], x_ref.at[at], load_sem.at[i])

    small = [
        pltpu.make_async_copy(w_hbm, d_ref, small_sem.at[0]),
        pltpu.make_async_copy(labels_hbm, labels_ref, small_sem.at[1]),
        pltpu.make_async_copy(weights_hbm, weights_ref, small_sem.at[2]),
    ]
    store_loss = pltpu.make_async_copy(loss_ref, loss_hbm, small_sem.at[3])
    small[0].start()
    for i in range(EARLY):
        load(i).start()
    small[1].start()
    small[2].start()

    barrier = pltpu.get_barrier_semaphore()
    greeted = [dp_peer(k) for k in range(1, RING * CORES)]
    greeted += [y_peer(k) for k in range(1, RING)] + [z_peer(k) for k in range(1, RING)]
    for peer in greeted:
        pl.semaphore_signal(barrier, inc=1, device_id=peer, device_id_type=MESH)

    small[0].wait()
    for i in range(EARLY, loads):
        load(i).start()
    wb_ref[...] = d_ref[...].astype(BF16)
    r_ref[...] = jnp.zeros_like(r_ref)
    sd_ref[...] = jnp.zeros_like(sd_ref)
    step_ref[...] = jnp.zeros_like(step_ref)
    def send(src, dst, send_sem, recv_sem, peer):
        copy = pltpu.make_async_remote_copy(
            src_ref=src,
            dst_ref=dst,
            send_sem=send_sem,
            recv_sem=recv_sem,
            device_id=peer,
            device_id_type=MESH,
        )
        copy.start()
        return copy

    def to_dp(ref, send_sem, recv_sem):
        for k in range(1, RING * CORES):
            send(ref.at[dp], ref.at[dp], send_sem, recv_sem, dp_peer(k))

    def to_ring(ref, at, send_sem, recv_sem, peer):
        for k in (2, 1, 3):
            send(ref.at[at], ref.at[at], send_sem, recv_sem, peer(k))

    def wait_all(ref, sem):
        pltpu.make_async_copy(ref, ref, sem).wait()

    def wait_group(ref, sem):
        wait_all(ref.at[pl.ds(0, ref.shape[0] - 1)], sem)

    at_1, peer_1 = (py, pz), (y_peer, z_peer)
    at_2, peer_2 = (pz, py), (z_peer, y_peer)

    block, sent = BLOCK, 0
    for start in range(0, rows, block):
        at = slice(start, start + block)
        for k in range(WIDE):
            load(start // block * WIDE + k).wait()
            over = slice(k * wide, (k + 1) * wide)
            part = dot(wb_ref[:, over], x_ref[at, over], 1, 1)
            acc_ref[:, at] = part if k == 0 else acc_ref[:, at] + part
        if start == 0:
            pl.semaphore_wait(barrier, len(greeted))
        while sent < 2 and (sent + 1) * half <= start + block:
            h, sent = sent, sent + 1
            l1_ref[h, at_1[h]] = acc_ref[:, h * half : (h + 1) * half]
            to_ring(l1_ref.at[h], at_1[h], f_send.at[0], f_recv.at[1, 0, h], peer_1[h])
    small[1].wait()
    small[2].wait()
    wt_ref[dp] = row_tile_sum(row_of(weights_ref, 0, rows).astype(F32))
    to_dp(wt_ref, wt_send.at[0], wt_recv.at[0])

    def turn_over(first, last):
        per_row = cols // block

        def one(i, _):
            row = pl.multiple_of((i // per_row) * block, block)
            col = pl.multiple_of(lax.rem(i, per_row) * block, block)
            xt_ref[pl.ds(col, block), pl.ds(row, block)] = x_ref[
                pl.ds(row, block), pl.ds(col, block)
            ].T
            return 0

        lax.fori_loop(first, last, one, 0)

    blocks = (rows // 512) * (cols // 512)

    turn_over(0, blocks // 2)
    for h in range(2):
        wait_group(l1_ref.at[h], f_recv.at[1, 0, h])
        l2_ref[h, at_2[h]] = ordered_sum(l1_ref.at[h], RING)
        to_ring(l2_ref.at[h], at_2[h], f_send.at[1], f_recv.at[1, 1, h], peer_2[h])
    turn_over(blocks // 2, blocks)
    wait_group(wt_ref, wt_recv.at[0])
    weight_total = whole_sum(ordered_sum(wt_ref, RING * CORES))

    loss_tile = None
    classes = lax.broadcasted_iota(jnp.int32, (w_hbm.shape[0], half), 0)
    for h in range(2):
        wait_group(l2_ref.at[h], f_recv.at[1, 1, h])
        at = slice(h * half, (h + 1) * half)
        logits = ordered_sum(l2_ref.at[h], RING)
        row_top = jnp.max(logits, axis=0, keepdims=True)
        shifted = jnp.exp(logits - row_top)
        summed = jnp.sum(shifted, axis=0, keepdims=True)
        class_prob = shifted / summed
        log_total = row_top + jnp.log(summed)
        row_weight = row_of(weights_ref, h * half, half).astype(F32)
        onehot = (row_of(labels_ref, h * half, half) == classes).astype(F32)
        picked = jnp.sum(logits * onehot, axis=0, keepdims=True)
        part = row_tile_sum(row_weight * (log_total - picked))
        loss_tile = part if loss_tile is None else loss_tile + part
        row_scale = row_weight / weight_total
        prob_ref[:, at] = class_prob
        rowscale_ref[:, at] = row_scale
        curv_ref[:, at] = (row_scale * (class_prob - onehot)).astype(BF16)
    q_ref[0, dp] = loss_tile
    to_dp(q_ref.at[0], q_send.at[0], q_recv.at[0])
    wait_all(l1_ref.at[:, pl.ds(1, RING - 1)], f_send.at[0])
    wait_all(l2_ref.at[:, pl.ds(1, RING - 1)], f_send.at[1])
    wait_group(wt_ref, wt_send.at[0])

    def wait_dp(slot):
        wait_group(q_ref.at[slot], q_recv.at[slot])
        wait_group(q_ref.at[slot], q_send.at[0])
        return whole_sum(ordered_sum(q_ref.at[slot], RING * CORES))

    one = jnp.ones((8, 128), F32)
    scal_ref[0] = one
    scal_ref[1] = one
    scal_ref[2] = one
    mine = core * own_cols
    theirs = (1 - core) * own_cols

    def iteration(it, _):
        slot = lax.rem(it, 2)

        ca_copies = []
        for s, (at, size) in enumerate(pieces):
            start = pl.multiple_of(theirs + at, 128)
            piece = pl.ds(at, size)
            ca_ref[slot, 0, :, piece] = dot(curv_ref[...], x_ref[:, pl.ds(start, size)], 1, 0).astype(
                BF16
            )
            ca_copies.append(
                send(
                    ca_ref.at[slot, 0, :, piece],
                    ca_ref.at[slot, 1, :, piece],
                    ca_send.at[0],
                    ca_recv.at[slot, s],
                    partner,
                )
            )
        for s, (at, size) in enumerate(pieces):
            start = pl.multiple_of(mine + at, 128)
            piece = pl.ds(at, size)
            part = dot(curv_ref[...], x_ref[:, pl.ds(start, size)], 1, 0)
            part_ref[:, piece] = part
            ca_copies[s].wait_recv()
            xs_ref[slot, px, :, piece] = (
                part_ref[:, piece] + ca_ref[slot, 1, :, piece].astype(F32)
            ).astype(BF16)
            to_ring(
                xs_ref.at[slot, :, :, piece], px, xs_send.at[0], xs_recv.at[slot, s], x_peer
            )

        reduced = wait_dp(slot)
        beta = scal_ref[0, 0:1, 0:1]
        res_norm = scal_ref[1, 0:1, 0:1]
        dir_norm = scal_ref[2, 0:1, 0:1]
        first = it == 0

        @pl.when(first)
        def _():
            loss_ref[...] = reduced / weight_total
            store_loss.start()

        step_size = jnp.where(first, 1.0, res_norm / (reduced + RIDGE_COEF * dir_norm))
        step_ref[...] = step_ref[...] + step_size * sd_ref[...]

        def advance(start, size, image):
            at = pl.ds(pl.multiple_of(start, 128), size)
            residual = r_ref[:, at]
            direction = residual + beta * d_ref[:, at]
            residual = residual - step_size * (image.astype(F32) + RIDGE_COEF * direction)
            r_ref[:, at] = residual
            d_ref[:, at] = direction
            tiles.append((tile_sum(residual * residual), tile_sum(residual * direction)))
            return residual.astype(BF16), xt_ref.at[at]

        tiles = []
        cb_copies = []

        def take_theirs(s):
            at, size = pieces[s]
            cb_copies[s].wait_recv()
            return advance(theirs + at, size, cb_ref[slot, 1, :, pl.ds(at, size)])

        for s, (at, size) in enumerate(pieces):
            piece = pl.ds(at, size)
            wait_group(xs_ref.at[slot, :, :, piece], xs_recv.at[slot, s])
            image = ordered_sum(xs_ref.at[slot, :, :, piece], RING).astype(BF16)
            cb_ref[slot, 0, :, piece] = image
            cb_copies.append(
                send(
                    cb_ref.at[slot, 0, :, piece],
                    cb_ref.at[slot, 1, :, piece],
                    cb_send.at[0],
                    cb_recv.at[slot, s],
                    partner,
                )
            )
            residual, turned = advance(mine + at, size, image)
            scores = dot(residual, turned[...], 1, 0)
            acc_ref[...] = scores if s == 0 else acc_ref[...] + scores
            if s > 0:
                residual, turned = take_theirs(s - 1)
                acc_ref[...] = acc_ref[...] + dot(residual, turned[...], 1, 0)
        residual, turned = take_theirs(len(pieces) - 1)

        for i in range(2):
            total = tiles[0][i]
            for both in tiles[1:]:
                total = total + both[i]
            g1_ref[slot, py, i] = total
        to_ring(g1_ref.at[slot], py, g_send.at[0], g_recv.at[slot, 0], y_peer)
        scores = (acc_ref[...] + dot(residual, turned[...], 1, 0)).astype(BF16)
        for h in range(2):
            f1_ref[slot, h, at_1[h]] = scores[:, h * half : (h + 1) * half]
            to_ring(f1_ref.at[slot, h], at_1[h], f_send.at[0], f_recv.at[slot, 0, h], peer_1[h])
        wait_group(g1_ref.at[slot], g_recv.at[slot, 0])
        g2_ref[slot, pz] = ordered_sum(g1_ref.at[slot], RING)
        to_ring(g2_ref.at[slot], pz, g_send.at[1], g_recv.at[slot, 1], z_peer)
        for h in range(2):
            wait_group(f1_ref.at[slot, h], f_recv.at[slot, 0, h])
            f2_ref[slot, h, at_2[h]] = ordered_sum(f1_ref.at[slot, h], RING).astype(BF16)
            to_ring(f2_ref.at[slot, h], at_2[h], f_send.at[1], f_recv.at[slot, 1, h], peer_2[h])
        wait_group(xs_ref.at[slot], xs_send.at[0])
        wait_all(ca_ref.at[slot, 0], ca_send.at[0])
        wait_all(cb_ref.at[slot, 0], cb_send.at[0])
        wait_all(f1_ref.at[slot, :, pl.ds(1, RING - 1)], f_send.at[0])
        wait_group(g1_ref.at[slot], g_send.at[0])

        wait_group(g2_ref.at[slot], g_recv.at[slot, 1])
        wait_group(g2_ref.at[slot], g_send.at[1])
        sums = ordered_sum(g2_ref.at[slot], RING)
        new_norm = whole_sum(sums[0])
        cross = whole_sum(sums[1])
        new_beta = jnp.where(first, 0.0, new_norm / (res_norm + NORM_GUARD))
        new_dir_norm = new_norm + new_beta * (2.0 * cross + new_beta * dir_norm)
        scal_ref[0] = jnp.broadcast_to(new_beta, (8, 128))
        scal_ref[1] = jnp.broadcast_to(new_norm, (8, 128))
        scal_ref[2] = jnp.broadcast_to(new_dir_norm, (8, 128))
        curvature = None
        for h in range(2):
            wait_group(f2_ref.at[slot, h], f_recv.at[slot, 1, h])
            at = slice(h * half, (h + 1) * half)
            scores = ordered_sum(f2_ref.at[slot, h], RING) + new_beta * sd_ref[:, at]
            sd_ref[:, at] = scores
            class_prob = prob_ref[:, at]
            mixed = jnp.sum(class_prob * scores, axis=0, keepdims=True)
            curv = (rowscale_ref[:, at] * class_prob * (scores - mixed)).astype(BF16)
            curv_ref[:, at] = curv
            part = tile_sum(scores * curv.astype(F32))
            curvature = part if curvature is None else curvature + part
        q_ref[1 - slot, dp] = curvature
        to_dp(q_ref.at[1 - slot], q_send.at[0], q_recv.at[1 - slot])
        wait_all(f2_ref.at[slot, :, pl.ds(1, RING - 1)], f_send.at[1])
        return 0

    lax.fori_loop(0, CG_ITERS, iteration, 0)

    store_loss.wait()
    last = CG_ITERS % 2
    reduced = wait_dp(last)
    step_size = scal_ref[1, 0:1, 0:1] / (reduced + RIDGE_COEF * scal_ref[2, 0:1, 0:1])
    step_ref[...] = step_ref[...] + step_size * sd_ref[...]


def on_device(features, weight, labels, sample_weight):
    arrays = (features, weight, labels, sample_weight)
    rows, cols = features.shape
    classes = weight.shape[0]
    half, own_cols = rows // 2, cols // CORES
    hbm = pl.BlockSpec(memory_space=pltpu.HBM)
    vmem = pl.BlockSpec(memory_space=pltpu.VMEM)
    dma = pltpu.SemaphoreType.DMA
    subs = len(SUBS)
    step, loss = pl.pallas_call(
        kernel,
        out_shape=(
            jax.ShapeDtypeStruct((classes, rows), F32),
            jax.ShapeDtypeStruct((1, 1), F32),
        ),
        in_specs=[hbm] * 4,
        out_specs=(vmem, hbm),
        scratch_shapes=[
            pltpu.VMEM((rows, cols), BF16),
            pltpu.VMEM((cols, rows), BF16),
            pltpu.VMEM((classes, cols), BF16),
            pltpu.VMEM((rows,), jnp.int32),
            pltpu.VMEM((rows,), jnp.int32),
            pltpu.VMEM((1, 1), F32),
            pltpu.VMEM((classes, cols), F32),
            pltpu.VMEM((classes, cols), F32),
            pltpu.VMEM((classes, rows), F32),
            pltpu.VMEM((1, rows), F32),
            pltpu.VMEM((classes, rows), BF16),
            pltpu.VMEM((classes, rows), F32),
            pltpu.VMEM((classes, rows), F32),
            pltpu.VMEM((classes, own_cols), F32),
            pltpu.VMEM((3, 8, 128), F32),
            pltpu.VMEM((2, RING, classes, half), F32),
            pltpu.VMEM((2, RING, classes, half), F32),
            pltpu.VMEM((2, 2, RING, classes, half), BF16),
            pltpu.VMEM((2, 2, RING, classes, half), BF16),
            pltpu.VMEM((2, RING, 2, 8, 128), F32),
            pltpu.VMEM((2, RING, 2, 8, 128), F32),
            pltpu.VMEM((2, 2, classes, own_cols), BF16),
            pltpu.VMEM((2, 2, classes, own_cols), BF16),
            pltpu.VMEM((2, RING, classes, own_cols), BF16),
            pltpu.VMEM((2, RING * CORES, 8, 128), F32),
            pltpu.VMEM((RING * CORES, 8, 128), F32),
            dma((rows // BLOCK * WIDE,)),
            dma((4,)),
            dma((2,)),
            dma((2, 2, 2)),
            dma((2,)),
            dma((2, 2)),
            dma((1,)),
            dma((2, subs)),
            dma((1,)),
            dma((2, subs)),
            dma((1,)),
            dma((2, subs)),
            dma((1,)),
            dma((2,)),
            dma((1,)),
            dma((1,)),
        ],
        compiler_params=pltpu.CompilerParams(
            collective_id=0, has_side_effects=True, vmem_limit_bytes=44 * 1024 * 1024
        ),
        name="newton_cg",
    )(*(pltpu.with_memory_space_constraint(a, pltpu.HBM) for a in arrays))
    return step.T, loss.reshape(())


def solution(mesh):
    in_specs = (P("dp", "feat"), P(None, "feat"), P("dp"), P("dp"))
    out_specs = (P("dp", None), P())
    return jax.shard_map(
        on_device, mesh=mesh, in_specs=in_specs, out_specs=out_specs, check_vma=False
    )
```

```python
import functools

import jax
import jax.numpy as jnp
from jax import lax
from jax.experimental import pallas as pl
from jax.experimental.pallas import tpu as pltpu
from jax.sharding import PartitionSpec as P

CG_ITERS = 4
RIDGE_COEF = 0.1
NORM_GUARD = 1e-06

RING = 4
CORES = 2
SUBS = (512, 768, 768)
BLOCK = 512
WIDE = 2
EARLY = 2
MESH = pl.DeviceIdType.MESH
F32 = jnp.float32
BF16 = jnp.bfloat16


def dot(a, b, contract_a, contract_b):
    return lax.dot_general(
        a, b, (((contract_a,), (contract_b,)), ((), ())), preferred_element_type=F32
    )


def tile_sum(value):
    total = None
    for i in range(0, value.shape[0], 8):
        for j in range(0, value.shape[1], 128):
            part = value[i : i + 8, j : j + 128]
            total = part if total is None else total + part
    return total


def row_tile_sum(value):
    total = None
    for j in range(0, value.shape[1], 128):
        part = value[:, j : j + 128]
        total = part if total is None else total + part
    first = lax.broadcasted_iota(jnp.int32, (8, 128), 0) == 0
    return jnp.where(first, jnp.broadcast_to(total, (8, 128)), 0.0)


def whole_sum(tile):
    return jnp.sum(jnp.sum(tile, axis=0, keepdims=True), axis=1, keepdims=True)


def row_of(ref, start, size):
    return ref[start : start + size].reshape(1, size)


def ordered_sum(ref, count):
    total = ref[0].astype(F32)
    for i in range(1, count):
        total = total + ref[i].astype(F32)
    return total


def kernel(
    x_hbm,
    w_hbm,
    labels_hbm,
    weights_hbm,
    step_ref,
    loss_hbm,
    x_ref,
    xt_ref,
    wb_ref,
    labels_ref,
    weights_ref,
    loss_ref,
    r_ref,
    d_ref,
    prob_ref,
    rowscale_ref,
    curv_ref,
    sd_ref,
    acc_ref,
    part_ref,
    scal_ref,
    l1_ref,
    l2_ref,
    f1_ref,
    f2_ref,
    g1_ref,
    g2_ref,
    ca_ref,
    cb_ref,
    xs_ref,
    q_ref,
    wt_ref,
    load_sem,
    small_sem,
    f_send,
    f_recv,
    g_send,
    g_recv,
    ca_send,
    ca_recv,
    cb_send,
    cb_recv,
    xs_send,
    xs_recv,
    q_send,
    q_recv,
    wt_send,
    wt_recv,
):
    dp = lax.axis_index("dp")
    ft = lax.axis_index("feat")
    px, core = dp // CORES, lax.rem(dp, CORES)
    pz, py = ft // RING, lax.rem(ft, RING)
    rows, cols = x_ref.shape
    half = rows // 2
    own_cols = cols // CORES
    wide = cols // WIDE
    loads = rows // BLOCK * WIDE
    pieces = [(sum(SUBS[:s]), SUBS[s]) for s in range(len(SUBS))]

    def turn(at, by):
        return lax.rem(at + by, RING)

    def y_peer(k):
        return (dp, pz * RING + turn(py, k))

    def z_peer(k):
        return (dp, turn(pz, k) * RING + py)

    def x_peer(k):
        return (turn(px, k) * CORES + core, ft)

    def dp_peer(k):
        return (lax.rem(dp + k, RING * CORES), ft)

    partner = (px * CORES + (1 - core), ft)

    def load(i):
        at = pl.ds(i // WIDE * BLOCK, BLOCK), pl.ds(i % WIDE * wide, wide)
        return pltpu.make_async_copy(x_hbm.at[at], x_ref.at[at], load_sem.at[i])

    small = [
        pltpu.make_async_copy(w_hbm, d_ref, small_sem.at[0]),
        pltpu.make_async_copy(labels_hbm, labels_ref, small_sem.at[1]),
        pltpu.make_async_copy(weights_hbm, weights_ref, small_sem.at[2]),
    ]
    store_loss = pltpu.make_async_copy(loss_ref, loss_hbm, small_sem.at[3])
    small[0].start()
    for i in range(EARLY):
        load(i).start()
    small[1].start()
    small[2].start()

    barrier = pltpu.get_barrier_semaphore()
    greeted = [dp_peer(k) for k in range(1, RING * CORES)]
    greeted += [y_peer(k) for k in range(1, RING)] + [z_peer(k) for k in range(1, RING)]
    for peer in greeted:
        pl.semaphore_signal(barrier, inc=1, device_id=peer, device_id_type=MESH)

    small[0].wait()
    for i in range(EARLY, loads):
        load(i).start()
    wb_ref[...] = d_ref[...].astype(BF16)
    r_ref[...] = jnp.zeros_like(r_ref)
    sd_ref[...] = jnp.zeros_like(sd_ref)
    step_ref[...] = jnp.zeros_like(step_ref)
    def send(src, dst, send_sem, recv_sem, peer):
        copy = pltpu.make_async_remote_copy(
            src_ref=src,
            dst_ref=dst,
            send_sem=send_sem,
            recv_sem=recv_sem,
            device_id=peer,
            device_id_type=MESH,
        )
        copy.start()
        return copy

    def to_dp(ref, send_sem, recv_sem):
        for k in range(1, RING * CORES):
            send(ref.at[dp], ref.at[dp], send_sem, recv_sem, dp_peer(k))

    def to_ring(ref, at, send_sem, recv_sem, peer):
        for k in (2, 1, 3):
            send(ref.at[at], ref.at[at], send_sem, recv_sem, peer(k))

    def wait_all(ref, sem):
        pltpu.make_async_copy(ref, ref, sem).wait()

    def wait_group(ref, sem):
        wait_all(ref.at[pl.ds(0, ref.shape[0] - 1)], sem)

    at_1, peer_1 = (py, pz), (y_peer, z_peer)
    at_2, peer_2 = (pz, py), (z_peer, y_peer)

    block, sent = BLOCK, 0
    for start in range(0, rows, block):
        at = slice(start, start + block)
        for k in range(WIDE):
            load(start // block * WIDE + k).wait()
            over = slice(k * wide, (k + 1) * wide)
            part = dot(wb_ref[:, over], x_ref[at, over], 1, 1)
            acc_ref[:, at] = part if k == 0 else acc_ref[:, at] + part
        if start == 0:
            pl.semaphore_wait(barrier, len(greeted))
        while sent < 2 and (sent + 1) * half <= start + block:
            h, sent = sent, sent + 1
            l1_ref[h, at_1[h]] = acc_ref[:, h * half : (h + 1) * half]
            to_ring(l1_ref.at[h], at_1[h], f_send.at[0], f_recv.at[1, 0, h], peer_1[h])
    small[1].wait()
    small[2].wait()
    wt_ref[dp] = row_tile_sum(row_of(weights_ref, 0, rows).astype(F32))
    to_dp(wt_ref, wt_send.at[0], wt_recv.at[0])

    def turn_over(first, last):
        per_row = cols // block

        def one(i, _):
            row = pl.multiple_of((i // per_row) * block, block)
            col = pl.multiple_of(lax.rem(i, per_row) * block, block)
            xt_ref[pl.ds(col, block), pl.ds(row, block)] = x_ref[
                pl.ds(row, block), pl.ds(col, block)
            ].T
            return 0

        lax.fori_loop(first, last, one, 0)

    blocks = (rows // 512) * (cols // 512)

    turn_over(0, blocks // 2)
    for h in range(2):
        wait_group(l1_ref.at[h], f_recv.at[1, 0, h])
        l2_ref[h, at_2[h]] = ordered_sum(l1_ref.at[h], RING)
        to_ring(l2_ref.at[h], at_2[h], f_send.at[1], f_recv.at[1, 1, h], peer_2[h])
    turn_over(blocks // 2, blocks)
    wait_group(wt_ref, wt_recv.at[0])
    weight_total = whole_sum(ordered_sum(wt_ref, RING * CORES))

    loss_tile = None
    classes = lax.broadcasted_iota(jnp.int32, (w_hbm.shape[0], half), 0)
    for h in range(2):
        wait_group(l2_ref.at[h], f_recv.at[1, 1, h])
        at = slice(h * half, (h + 1) * half)
        logits = ordered_sum(l2_ref.at[h], RING)
        row_top = jnp.max(logits, axis=0, keepdims=True)
        shifted = jnp.exp(logits - row_top)
        summed = jnp.sum(shifted, axis=0, keepdims=True)
        class_prob = shifted / summed
        log_total = row_top + jnp.log(summed)
        row_weight = row_of(weights_ref, h * half, half).astype(F32)
        onehot = (row_of(labels_ref, h * half, half) == classes).astype(F32)
        picked = jnp.sum(logits * onehot, axis=0, keepdims=True)
        part = row_tile_sum(row_weight * (log_total - picked))
        loss_tile = part if loss_tile is None else loss_tile + part
        row_scale = row_weight / weight_total
        prob_ref[:, at] = class_prob
        rowscale_ref[:, at] = row_scale
        curv_ref[:, at] = (row_scale * (class_prob - onehot)).astype(BF16)
    q_ref[0, dp] = loss_tile
    to_dp(q_ref.at[0], q_send.at[0], q_recv.at[0])
    wait_all(l1_ref.at[:, pl.ds(1, RING - 1)], f_send.at[0])
    wait_all(l2_ref.at[:, pl.ds(1, RING - 1)], f_send.at[1])
    wait_group(wt_ref, wt_send.at[0])

    def wait_dp(slot):
        wait_group(q_ref.at[slot], q_recv.at[slot])
        wait_group(q_ref.at[slot], q_send.at[0])
        return whole_sum(ordered_sum(q_ref.at[slot], RING * CORES))

    one = jnp.ones((8, 128), F32)
    scal_ref[0] = one
    scal_ref[1] = one
    scal_ref[2] = one
    mine = core * own_cols
    theirs = (1 - core) * own_cols

    def iteration(it, _):
        slot = lax.rem(it, 2)

        ca_copies = []
        for s, (at, size) in enumerate(pieces):
            start = pl.multiple_of(theirs + at, 128)
            piece = pl.ds(at, size)
            ca_ref[slot, 0, :, piece] = dot(curv_ref[...], x_ref[:, pl.ds(start, size)], 1, 0).astype(
                BF16
            )
            ca_copies.append(
                send(
                    ca_ref.at[slot, 0, :, piece],
                    ca_ref.at[slot, 1, :, piece],
                    ca_send.at[0],
                    ca_recv.at[slot, s],
                    partner,
                )
            )
        for s, (at, size) in enumerate(pieces):
            start = pl.multiple_of(mine + at, 128)
            piece = pl.ds(at, size)
            part = dot(curv_ref[...], x_ref[:, pl.ds(start, size)], 1, 0)
            part_ref[:, piece] = part
            ca_copies[s].wait_recv()
            xs_ref[slot, px, :, piece] = (
                part_ref[:, piece] + ca_ref[slot, 1, :, piece].astype(F32)
            ).astype(BF16)
            to_ring(
                xs_ref.at[slot, :, :, piece], px, xs_send.at[0], xs_recv.at[slot, s], x_peer
            )

        reduced = wait_dp(slot)
        beta = scal_ref[0, 0:1, 0:1]
        res_norm = scal_ref[1, 0:1, 0:1]
        dir_norm = scal_ref[2, 0:1, 0:1]
        first = it == 0

        @pl.when(first)
        def _():
            loss_ref[...] = reduced / weight_total
            store_loss.start()

        step_size = jnp.where(first, 1.0, res_norm / (reduced + RIDGE_COEF * dir_norm))
        step_ref[...] = step_ref[...] + step_size * sd_ref[...]

        def advance(start, size, image):
            at = pl.ds(pl.multiple_of(start, 128), size)
            residual = r_ref[:, at]
            direction = residual + beta * d_ref[:, at]
            residual = residual - step_size * (image.astype(F32) + RIDGE_COEF * direction)
            r_ref[:, at] = residual
            d_ref[:, at] = direction
            tiles.append((tile_sum(residual * residual), tile_sum(residual * direction)))
            return residual.astype(BF16), xt_ref.at[at]

        tiles = []
        cb_copies = []

        def take_theirs(s):
            at, size = pieces[s]
            cb_copies[s].wait_recv()
            return advance(theirs + at, size, cb_ref[slot, 1, :, pl.ds(at, size)])

        for s, (at, size) in enumerate(pieces):
            piece = pl.ds(at, size)
            wait_group(xs_ref.at[slot, :, :, piece], xs_recv.at[slot, s])
            image = ordered_sum(xs_ref.at[slot, :, :, piece], RING).astype(BF16)
            cb_ref[slot, 0, :, piece] = image
            cb_copies.append(
                send(
                    cb_ref.at[slot, 0, :, piece],
                    cb_ref.at[slot, 1, :, piece],
                    cb_send.at[0],
                    cb_recv.at[slot, s],
                    partner,
                )
            )
            residual, turned = advance(mine + at, size, image)
            scores = dot(residual, turned[...], 1, 0)
            acc_ref[...] = scores if s == 0 else acc_ref[...] + scores
            if s > 0:
                residual, turned = take_theirs(s - 1)
                acc_ref[...] = acc_ref[...] + dot(residual, turned[...], 1, 0)
        residual, turned = take_theirs(len(pieces) - 1)

        for i in range(2):
            total = tiles[0][i]
            for both in tiles[1:]:
                total = total + both[i]
            g1_ref[slot, py, i] = total
        to_ring(g1_ref.at[slot], py, g_send.at[0], g_recv.at[slot, 0], y_peer)
        scores = (acc_ref[...] + dot(residual, turned[...], 1, 0)).astype(BF16)
        for h in range(2):
            f1_ref[slot, h, at_1[h]] = scores[:, h * half : (h + 1) * half]
            to_ring(f1_ref.at[slot, h], at_1[h], f_send.at[0], f_recv.at[slot, 0, h], peer_1[h])
        wait_group(g1_ref.at[slot], g_recv.at[slot, 0])
        g2_ref[slot, pz] = ordered_sum(g1_ref.at[slot], RING)
        to_ring(g2_ref.at[slot], pz, g_send.at[1], g_recv.at[slot, 1], z_peer)
        for h in range(2):
            wait_group(f1_ref.at[slot, h], f_recv.at[slot, 0, h])
            f2_ref[slot, h, at_2[h]] = ordered_sum(f1_ref.at[slot, h], RING).astype(BF16)
            to_ring(f2_ref.at[slot, h], at_2[h], f_send.at[1], f_recv.at[slot, 1, h], peer_2[h])
        wait_group(xs_ref.at[slot], xs_send.at[0])
        wait_all(ca_ref.at[slot, 0], ca_send.at[0])
        wait_all(cb_ref.at[slot, 0], cb_send.at[0])
        wait_all(f1_ref.at[slot, :, pl.ds(1, RING - 1)], f_send.at[0])
        wait_group(g1_ref.at[slot], g_send.at[0])

        wait_group(g2_ref.at[slot], g_recv.at[slot, 1])
        wait_group(g2_ref.at[slot], g_send.at[1])
        sums = ordered_sum(g2_ref.at[slot], RING)
        new_norm = whole_sum(sums[0])
        cross = whole_sum(sums[1])
        new_beta = jnp.where(first, 0.0, new_norm / (res_norm + NORM_GUARD))
        new_dir_norm = new_norm + new_beta * (2.0 * cross + new_beta * dir_norm)
        scal_ref[0] = jnp.broadcast_to(new_beta, (8, 128))
        scal_ref[1] = jnp.broadcast_to(new_norm, (8, 128))
        scal_ref[2] = jnp.broadcast_to(new_dir_norm, (8, 128))
        curvature = None
        for h in range(2):
            wait_group(f2_ref.at[slot, h], f_recv.at[slot, 1, h])
            at = slice(h * half, (h + 1) * half)
            scores = ordered_sum(f2_ref.at[slot, h], RING) + new_beta * sd_ref[:, at]
            sd_ref[:, at] = scores
            class_prob = prob_ref[:, at]
            mixed = jnp.sum(class_prob * scores, axis=0, keepdims=True)
            curv = (rowscale_ref[:, at] * class_prob * (scores - mixed)).astype(BF16)
            curv_ref[:, at] = curv
            part = tile_sum(scores * curv.astype(F32))
            curvature = part if curvature is None else curvature + part
        q_ref[1 - slot, dp] = curvature
        to_dp(q_ref.at[1 - slot], q_send.at[0], q_recv.at[1 - slot])
        wait_all(f2_ref.at[slot, :, pl.ds(1, RING - 1)], f_send.at[1])
        return 0

    lax.fori_loop(0, CG_ITERS, iteration, 0)

    store_loss.wait()
    last = CG_ITERS % 2
    reduced = wait_dp(last)
    step_size = scal_ref[1, 0:1, 0:1] / (reduced + RIDGE_COEF * scal_ref[2, 0:1, 0:1])
    step_ref[...] = step_ref[...] + step_size * sd_ref[...]


def on_device(features, weight, labels, sample_weight):
    arrays = (features, weight, labels, sample_weight)
    rows, cols = features.shape
    classes = weight.shape[0]
    half, own_cols = rows // 2, cols // CORES
    hbm = pl.BlockSpec(memory_space=pltpu.HBM)
    vmem = pl.BlockSpec(memory_space=pltpu.VMEM)
    dma = pltpu.SemaphoreType.DMA
    subs = len(SUBS)
    step, loss = pl.pallas_call(
        kernel,
        out_shape=(
            jax.ShapeDtypeStruct((classes, rows), F32),
            jax.ShapeDtypeStruct((1, 1), F32),
        ),
        in_specs=[hbm] * 4,
        out_specs=(vmem, hbm),
        scratch_shapes=[
            pltpu.VMEM((rows, cols), BF16),
            pltpu.VMEM((cols, rows), BF16),
            pltpu.VMEM((classes, cols), BF16),
            pltpu.VMEM((rows,), jnp.int32),
            pltpu.VMEM((rows,), jnp.int32),
            pltpu.VMEM((1, 1), F32),
            pltpu.VMEM((classes, cols), F32),
            pltpu.VMEM((classes, cols), F32),
            pltpu.VMEM((classes, rows), F32),
            pltpu.VMEM((1, rows), F32),
            pltpu.VMEM((classes, rows), BF16),
            pltpu.VMEM((classes, rows), F32),
            pltpu.VMEM((classes, rows), F32),
            pltpu.VMEM((classes, own_cols), F32),
            pltpu.VMEM((3, 8, 128), F32),
            pltpu.VMEM((2, RING, classes, half), F32),
            pltpu.VMEM((2, RING, classes, half), F32),
            pltpu.VMEM((2, 2, RING, classes, half), BF16),
            pltpu.VMEM((2, 2, RING, classes, half), BF16),
            pltpu.VMEM((2, RING, 2, 8, 128), F32),
            pltpu.VMEM((2, RING, 2, 8, 128), F32),
            pltpu.VMEM((2, 2, classes, own_cols), BF16),
            pltpu.VMEM((2, 2, classes, own_cols), BF16),
            pltpu.VMEM((2, RING, classes, own_cols), BF16),
            pltpu.VMEM((2, RING * CORES, 8, 128), F32),
            pltpu.VMEM((RING * CORES, 8, 128), F32),
            dma((rows // BLOCK * WIDE,)),
            dma((4,)),
            dma((2,)),
            dma((2, 2, 2)),
            dma((2,)),
            dma((2, 2)),
            dma((1,)),
            dma((2, subs)),
            dma((1,)),
            dma((2, subs)),
            dma((1,)),
            dma((2, subs)),
            dma((1,)),
            dma((2,)),
            dma((1,)),
            dma((1,)),
        ],
        compiler_params=pltpu.CompilerParams(
            collective_id=0, has_side_effects=True, vmem_limit_bytes=44 * 1024 * 1024
        ),
        name="newton_cg",
    )(*(pltpu.with_memory_space_constraint(a, pltpu.HBM) for a in arrays))
    return step.T, loss.reshape(())


def solution(mesh):
    in_specs = (P("dp", "feat"), P(None, "feat"), P("dp"), P("dp"))
    out_specs = (P("dp", None), P())
    return jax.shard_map(
        on_device, mesh=mesh, in_specs=in_specs, out_specs=out_specs, check_vma=False
    )
```
